32 devices in a mesh: grp: 4 (over y, x), slab: 8 (over z, core).
Axes of the slice: x: 2, y: 2, z: 4, core: 2. Of those that a mesh axis runs over, the one named last changes fastest.
Arguments:
- templates: float32 [4, 8, 512, 512], P('grp', None, 'slab'), may hold values from -6 to 6
- momentum: float32 [4, 8, 512, 512], P('grp', None, 'slab'), may hold values from -6 to 6
- subjects: float32 [4, 8, 512, 512], P('grp', None, 'slab'), may hold values from -6 to 6
- smooth_x: float32 [512, 512], replicated, may hold values from 0 to 1
- smooth_y: float32 [512, 512], replicated, may hold values from 0 to 1
- smooth_z: float32 [8, 8], replicated, may hold values from 0 to 1.5
- owned_block: int32 [4], replicated, may hold values from 0 to 3, each once
Outputs:
- final_image: float32 [4, 8, 512, 512], P('grp', None, 'slab')
- final_momentum: float32 [4, 8, 512, 512], P('grp', None, 'slab')
- center_owned: float32 [4, 2, 512, 512], P('grp', None, 'slab')
- new_templates: float32 [4, 8, 512, 512], P('grp', None, 'slab')
The draws below stay inside these ranges and needn't reach their ends.
Inputs may be any that keep to these rules, and one draw needn't show every extreme that they name: `owned_block`: a permutation: every block has exactly one owning group.
All inputs are finite; a program needn't handle non-finite values.
Results may differ from the reference program's by a relative error of at most 0.0001.
Values sent between devices are 32-bit elements; how exact they have to be, the bound alone decides.
A program may use at most 64 MiB of HBM per device.

```python
import math
import jax
import jax.numpy as jnp
from jax import lax

N = 512
BLK_PLANES = 2
STEPS = 2
GROUPS = 4
PLANES = 8
ELL = 64
ELL_Z = 1


def kernel_matrix(key, order, length):
    index = jnp.arange(order)
    distance = jnp.abs(index[:, None] - index[None, :]).astype(jnp.float32)
    factor = jax.random.uniform(key, (order, order), jnp.float32, 0.5, 1.5)
    return jnp.exp(-distance / length) * factor / math.sqrt(length)


def draw_smooth_x(key, part):
    return kernel_matrix(jax.random.fold_in(key, 11), N, ELL)


def draw_smooth_y(key, part):
    return kernel_matrix(jax.random.fold_in(key, 23), N, ELL)


def draw_smooth_z(key, part):
    return kernel_matrix(jax.random.fold_in(key, 37), PLANES, ELL_Z)


def steps_of(own_key, shape, split, smallest, high):
    def one(dim, parts):
        steps = jax.random.uniform(jax.random.fold_in(jax.random.fold_in(own_key, 6), dim), (parts,), jnp.float32, smallest / len(split), high / len(split))
        return jnp.repeat(jnp.exp(steps), shape[dim] // parts).reshape((-1,) + (1,) * (len(shape) - dim - 1))

    level = one(*split[0])
    for cut in split[1:]:
        level = level * one(*cut)
    return level


def scatter_about(rng, dims, width, limit, split=(), held_as=jnp.bfloat16):
    entries = jax.random.normal(rng, dims, jnp.float32) * width
    if len(split) > 0:
        entries = steps_of(rng, dims, split, -0.22, 0.18) * entries
    return jnp.clip(entries, min=-limit, max=limit).astype(held_as)


def setup_inputs(seed: int = 0) -> dict:
    seeds = jax.random.split(jax.random.key(seed), 8)
    templates = scatter_about(seeds[0], (GROUPS, PLANES, N, N), 1.0, 6.0, ((0, 4), (2, 8)), jnp.float32)
    momentum = scatter_about(seeds[1], (GROUPS, PLANES, N, N), 1.0, 6.0, ((0, 4), (2, 8)), jnp.float32)
    subjects = scatter_about(seeds[2], (GROUPS, PLANES, N, N), 1.0, 6.0, ((0, 4), (2, 8)), jnp.float32)
    smooth_x = draw_smooth_x(jax.random.fold_in(seeds[7], 71), 0)
    smooth_y = draw_smooth_y(jax.random.fold_in(seeds[7], 71), 0)
    smooth_z = draw_smooth_z(jax.random.fold_in(seeds[7], 71), 0)
    owned_block = jax.random.permutation(seeds[6], GROUPS).astype(jnp.int32)
    return dict(templates=templates, momentum=momentum, subjects=subjects, smooth_x=smooth_x, smooth_y=smooth_y, smooth_z=smooth_z, owned_block=owned_block)


learn_rate = 0.5
pull_weight = 0.5


def diff_cols(field):
    zeros = jnp.zeros_like(field[..., :1])
    padded = jnp.concatenate([zeros, field, zeros], axis=-1)
    return (padded[..., 2:] - padded[..., :-2]) * 0.5


def diff_rows(field):
    zeros = jnp.zeros_like(field[..., :1, :])
    padded = jnp.concatenate([zeros, field, zeros], axis=-2)
    return (padded[..., 2:, :] - padded[..., :-2, :]) * 0.5


def diff_planes(field):
    zeros = jnp.zeros_like(field[..., :1, :, :])
    padded = jnp.concatenate([zeros, field, zeros], axis=-3)
    return (padded[..., 2:, :, :] - padded[..., :-2, :, :]) * 0.5


def smooth(field, smooth_x, smooth_y, smooth_z):
    across = jnp.einsum('ij,gjyx->giyx', smooth_z, field, precision=lax.Precision.HIGHEST)
    along = jnp.einsum('ij,gpyj->gpyi', smooth_x, across, precision=lax.Precision.HIGHEST)
    return jnp.einsum('ij,gpjx->gpix', smooth_y, along, precision=lax.Precision.HIGHEST)


def reference(templates, momentum, subjects, smooth_x, smooth_y, smooth_z, owned_block):
    time_step = 1.0 / STEPS
    image = templates
    moment = momentum
    for section in range(STEPS):
        grad_cols = diff_cols(image)
        grad_rows = diff_rows(image)
        grad_planes = diff_planes(image)
        vel_cols = -smooth(moment * grad_cols, smooth_x, smooth_y, smooth_z)
        vel_rows = -smooth(moment * grad_rows, smooth_x, smooth_y, smooth_z)
        vel_planes = -smooth(moment * grad_planes, smooth_x, smooth_y, smooth_z)
        new_image = image - time_step * (vel_cols * grad_cols + vel_rows * grad_rows + vel_planes * grad_planes)
        new_moment = moment - time_step * (diff_cols(moment * vel_cols) + diff_rows(moment * vel_rows) + diff_planes(moment * vel_planes))
        image = new_image
        moment = new_moment
    update = templates - learn_rate * (image - subjects)
    center = jnp.sum(update, axis=0) / GROUPS
    blocks = center.reshape(GROUPS, BLK_PLANES, N, N)
    center_owned = jnp.take(blocks, owned_block.astype(jnp.int32), axis=0)
    new_templates = update + pull_weight * (center[None] - update)
    return image, moment, center_owned, new_templates
```

```python
import functools

import jax
import jax.numpy as jnp
from jax import lax
from jax.experimental import pallas as pl
from jax.experimental.pallas import tpu as pltpu
from jax.sharding import PartitionSpec as P

STEPS = 2
EDGE = 8
VMEM_BYTES = 60 * 2**20
GATHER_BYTES = 16 * 2**20


learn_rate = 0.5
pull_weight = 0.5


def with_halo(cells, sides, width):
    for axis, dim in sides:
        count = lax.axis_size(axis)
        ends = count - 1
        head = lax.slice_in_dim(cells, 0, width, axis=dim)
        tail = lax.slice_in_dim(cells, cells.shape[dim] - width, cells.shape[dim], axis=dim)
        cells = jnp.concatenate(
            [
                lax.ppermute(tail, axis, [(i, (i + 1) % count) for i in range(ends)]),
                cells,
                lax.ppermute(head, axis, [((i + 1) % count, i) for i in range(ends)]),
            ],
            axis=dim,
        )
    return cells


def diff_cols(field):
    zeros = jnp.zeros_like(field[..., :1])
    padded = jnp.concatenate([zeros, field, zeros], axis=-1)
    return (padded[..., 2:] - padded[..., :-2]) * 0.5


def diff_planes(field):
    zeros = jnp.zeros_like(field[..., :1, :, :])
    padded = jnp.concatenate([zeros, field, zeros], axis=-3)
    return (padded[..., 2:, :, :] - padded[..., :-2, :, :]) * 0.5


def smooth_planes(field, smooth_z):
    return jnp.einsum("ij,cjyx->ciyx", smooth_z, field, precision=lax.Precision.HIGHEST)


def smooth_plane(field, smooth_x, smooth_y):
    along = jnp.einsum("ij,cpyj->cpyi", smooth_x, field, precision=lax.Precision.HIGHEST)
    return jnp.einsum("ij,cpjx->cpix", smooth_y, along, precision=lax.Precision.HIGHEST)


def diff_rows(field):
    zeros = jnp.zeros_like(field[..., :1, :])
    padded = jnp.concatenate([zeros, field, zeros], axis=-2)
    return (padded[..., 2:, :] - padded[..., :-2, :]) * 0.5


def rows_of(field, start, count):
    return lax.dynamic_slice_in_dim(field, start, count, field.ndim - 2)


def halve(field):
    high = field.astype(jnp.bfloat16)
    return high, (field - high.astype(jnp.float32)).astype(jnp.bfloat16)


def dot3(left, right):
    mul = lambda a, b: jnp.dot(a, b, preferred_element_type=jnp.float32)
    return mul(left[0], right[0]) + (mul(left[0], right[1]) + mul(left[1], right[0]))


def central(field, axis):
    size = field.shape[axis]
    place = lax.broadcasted_iota(jnp.int32, field.shape, axis)
    after = jnp.where(place == size - 1, 0.0, pltpu.roll(field, size - 1, axis))
    before = jnp.where(place == 0, 0.0, pltpu.roll(field, 1, axis))
    return (after - before) * 0.5


def plane_grads(plane, planes, below, here, above):
    over = jnp.where(plane == planes - 1, 0.0, above)
    under = jnp.where(plane == 0, 0.0, below)
    return central(here, 1), central(here, 0), (over - under) * 0.5


def smooth_fields(grads, moment, fields, matrices, store):
    rows_high, rows_low, cols_high, cols_low = matrices
    for at, grad in enumerate(grads):
        fields[at] = moment * grad

    @pl.loop(0, 3)
    def _(at):
        along = dot3((rows_high[...], rows_low[...]), halve(fields[at]))
        store(at, dot3(halve(along), (cols_high[...], cols_low[...])))


def split_matrices(rows_ref, cols_ref, matrices):
    matrices[0][...], matrices[1][...] = halve(rows_ref[...])
    matrices[2][...], matrices[3][...] = halve(cols_ref[...])


def full_kernel(
    planes, step, smooth_z, below, here, above, m_below, m_here, m_above, rows_ref, cols_ref,
    image_out, moment_out, vel, fields, *matrices,
):
    at = pl.program_id(0)
    plane = at % planes

    @pl.when(at == 0)
    def _():
        split_matrices(rows_ref, cols_ref, matrices)

    @pl.when(at < planes)
    def _():
        grads = plane_grads(plane, planes, below[...], here[...], above[...])

        def store(field, value):
            vel[field, plane] = value

        smooth_fields(grads, m_here[...], fields, matrices, store)

    @pl.when(at == planes)
    def _():
        rows = vel.shape[2] // 8

        @pl.loop(0, 3 * rows)
        def _(turn):
            field = turn // rows
            span = pl.ds(pl.multiple_of((turn % rows) * 8, 8), 8)
            held = [vel[field, j, span, :] for j in range(planes)]
            for i in range(planes):
                vel[field, i, span, :] = -sum(smooth_z[i, j] * held[j] for j in range(planes))

    @pl.when(at >= planes)
    def _():
        grads = plane_grads(plane, planes, below[...], here[...], above[...])
        moment = m_here[...]
        moved = [vel[field, plane] for field in range(3)]
        image_out[...] = here[...] - step * sum(v * g for v, g in zip(moved, grads))
        over = m_above[...] * vel[2, jnp.minimum(plane + 1, planes - 1)]
        under = m_below[...] * vel[2, jnp.maximum(plane - 1, 0)]
        over = jnp.where(plane == planes - 1, 0.0, over)
        under = jnp.where(plane == 0, 0.0, under)
        moment_out[...] = moment - step * (
            central(moment * moved[0], 1) + central(moment * moved[1], 0) + (over - under) * 0.5
        )


def part_kernel(
    planes, below, here, above, m_here, rows_ref, cols_ref, vel_out, fields, *matrices
):
    plane = pl.program_id(0)

    @pl.when(plane == 0)
    def _():
        split_matrices(rows_ref, cols_ref, matrices)

    grads = plane_grads(plane, planes, below[...], here[...], above[...])

    def store(field, value):
        vel_out[field] = value

    smooth_fields(grads, m_here[...], fields, matrices, store)


def plane_spec(planes, rows, cols, which, shift):
    def index(at):
        return which, jnp.clip(at % planes + shift, 0, planes - 1), 0, 0

    return pl.BlockSpec((None, None, rows, cols), index)


def matrix_scratch(rows, inner, cols):
    kinds = [(rows, inner), (rows, inner), (cols, cols), (cols, cols)]
    return [pltpu.VMEM(kind, jnp.bfloat16) for kind in kinds]


def whole_spec(shape):
    return pl.BlockSpec(shape, lambda at: (0,) * len(shape))


def full_step(state, smooth_x, smooth_y, smooth_z, step):
    _, planes, rows, cols = state.shape
    spec = lambda which, shift: plane_spec(planes, rows, cols, which, shift)
    late = pl.BlockSpec((None, rows, cols), lambda at: (jnp.maximum(at - planes, 0), 0, 0))
    out = jax.ShapeDtypeStruct((planes, rows, cols), jnp.float32)
    return pl.pallas_call(
        functools.partial(full_kernel, planes, step),
        grid=(2 * planes,),
        out_shape=(out, out),
        in_specs=[pl.BlockSpec(memory_space=pltpu.SMEM)]
        + [spec(which, shift) for which in (0, 1) for shift in (-1, 0, 1)]
        + [whole_spec(smooth_y.shape), whole_spec(smooth_x.shape)],
        out_specs=(late, late),
        scratch_shapes=[
            pltpu.VMEM((3, planes, rows, cols), jnp.float32),
            pltpu.VMEM((3, rows, cols), jnp.float32),
        ]
        + matrix_scratch(rows, rows, cols),
        compiler_params=pltpu.CompilerParams(vmem_limit_bytes=VMEM_BYTES),
    )(smooth_z, *[state] * 6, smooth_y, smooth_x.T)


def part_smooth(image, moment, smooth_x, smooth_y):
    planes, rows, cols = image.shape
    span = smooth_y.shape[0]
    spec = lambda shift: pl.BlockSpec(
        (None, rows, cols), lambda at: (jnp.clip(at + shift, 0, planes - 1), 0, 0)
    )
    return pl.pallas_call(
        functools.partial(part_kernel, planes),
        grid=(planes,),
        out_shape=jax.ShapeDtypeStruct((3, planes, span, cols), jnp.float32),
        in_specs=[spec(-1), spec(0), spec(1), spec(0)]
        + [whole_spec(smooth_y.shape), whole_spec(smooth_x.shape)],
        out_specs=pl.BlockSpec((3, None, span, cols), lambda at: (0, at, 0, 0)),
        scratch_shapes=[pltpu.VMEM((3, rows, cols), jnp.float32)]
        + matrix_scratch(span, rows, cols),
        compiler_params=pltpu.CompilerParams(vmem_limit_bytes=VMEM_BYTES),
    )(image, image, image, moment, smooth_y, smooth_x.T)


def on_device_gathered(templates, momentum, subjects, smooth_x, smooth_y, smooth_z, owned_block):
    time_step = 1.0 / STEPS
    own = templates.shape[2]
    total = smooth_y.shape[0]
    index = lax.axis_index("slab")
    state = lax.all_gather(
        jnp.concatenate([templates, momentum], axis=0), "slab", axis=2, tiled=True
    )
    for section in range(STEPS - 1):
        image, moment = full_step(state, smooth_x, smooth_y, smooth_z, time_step)
        if section < STEPS - 2:
            state = jnp.stack([image, moment])
    span = own + 2 * EDGE
    first = jnp.clip(index * own - EDGE, 0, total - span)
    inner = index * own - first
    vel = part_smooth(image, moment, smooth_x, rows_of(smooth_y, first, span))
    vel = -smooth_planes(vel, smooth_z)
    image, moment = rows_of(image, first, span), rows_of(moment, first, span)
    grads = [diff_cols(image), diff_rows(image), diff_planes(image)]
    new_image = image - time_step * sum(v * g for v, g in zip(vel, grads))
    new_moment = moment - time_step * (
        diff_cols(moment * vel[0]) + diff_rows(moment * vel[1]) + diff_planes(moment * vel[2])
    )
    image, moment = rows_of(new_image, inner, own), rows_of(new_moment, inner, own)
    return finish(image, moment, templates, subjects, owned_block)


def on_device(templates, momentum, subjects, smooth_x, smooth_y, smooth_z, owned_block):
    time_step = 1.0 / STEPS
    image = templates[0]
    moment = momentum[0]
    for section in range(STEPS):
        image_rows = with_halo(image, (("slab", 1),), 1)
        grad_rows = (image_rows[:, 2:, :] - image_rows[:, :-2, :]) * 0.5
        grad_cols = diff_cols(image)
        grad_planes = diff_planes(image)
        pushing = smooth_planes(
            jnp.stack([moment * grad_cols, moment * grad_rows, moment * grad_planes]), smooth_z
        )
        plane_fields = lax.all_to_all(pushing, "slab", split_axis=1, concat_axis=2, tiled=True)
        plane_vel = -smooth_plane(plane_fields, smooth_x, smooth_y)
        velocity = lax.all_to_all(plane_vel, "slab", split_axis=2, concat_axis=1, tiled=True)
        flux_edge = with_halo(moment * velocity[1], (("slab", 1),), 1)
        flux_rows = (flux_edge[:, 2:, :] - flux_edge[:, :-2, :]) * 0.5
        new_image = image - time_step * (
            velocity[0] * grad_cols + velocity[1] * grad_rows + velocity[2] * grad_planes
        )
        new_moment = moment - time_step * (
            diff_cols(moment * velocity[0]) + flux_rows + diff_planes(moment * velocity[2])
        )
        image = new_image
        moment = new_moment
    return finish(image, moment, templates, subjects, owned_block)


def finish(image, moment, templates, subjects, owned_block):
    groups = lax.axis_size("grp")
    update = templates[0] - learn_rate * (image - subjects[0])
    planes_all = update.shape[0]
    block_planes = planes_all // groups
    center = lax.psum(update, "grp") / groups
    owned_index = owned_block[lax.axis_index("grp")]
    owned_out = lax.dynamic_slice_in_dim(center, owned_index * block_planes, block_planes, 0)[None]
    new_template = update + pull_weight * (center - update)
    return (image[None], moment[None], owned_out, new_template[None])


def solution(mesh):
    def body(*args):
        templates, smooth_y = args[0], args[4]
        gathered = 2 * 4 * templates.shape[1] * templates.shape[3] * smooth_y.shape[0]
        return (on_device_gathered if gathered <= GATHER_BYTES else on_device)(*args)

    return jax.shard_map(
        body,
        mesh=mesh,
        in_specs=(
            P("grp", None, "slab", None),
            P("grp", None, "slab", None),
            P("grp", None, "slab", None),
            P(),
            P(),
            P(),
            P(),
        ),
        out_specs=(
            P("grp", None, "slab", None),
            P("grp", None, "slab", None),
            P("grp", None, "slab", None),
            P("grp", None, "slab", None),
        ),
        check_vma=False,
    )
```

```python
import functools

import jax
import jax.numpy as jnp
from jax import lax
from jax.experimental import pallas as pl
from jax.experimental.pallas import tpu as pltpu
from jax.sharding import PartitionSpec as P

STEPS = 2
EDGE = 8
CUTS = (3, 5, 7)
VMEM_BYTES = 60 * 2**20
GATHER_BYTES = 16 * 2**20


learn_rate = 0.5
pull_weight = 0.5


def with_halo(cells, sides, width):
    for axis, dim in sides:
        count = lax.axis_size(axis)
        ends = count - 1
        head = lax.slice_in_dim(cells, 0, width, axis=dim)
        tail = lax.slice_in_dim(cells, cells.shape[dim] - width, cells.shape[dim], axis=dim)
        cells = jnp.concatenate(
            [
                lax.ppermute(tail, axis, [(i, (i + 1) % count) for i in range(ends)]),
                cells,
                lax.ppermute(head, axis, [((i + 1) % count, i) for i in range(ends)]),
            ],
            axis=dim,
        )
    return cells


def diff_cols(field):
    zeros = jnp.zeros_like(field[..., :1])
    padded = jnp.concatenate([zeros, field, zeros], axis=-1)
    return (padded[..., 2:] - padded[..., :-2]) * 0.5


def diff_planes(field):
    zeros = jnp.zeros_like(field[..., :1, :, :])
    padded = jnp.concatenate([zeros, field, zeros], axis=-3)
    return (padded[..., 2:, :, :] - padded[..., :-2, :, :]) * 0.5


def smooth_planes(field, smooth_z):
    return jnp.einsum("ij,cjyx->ciyx", smooth_z, field, precision=lax.Precision.HIGHEST)


def smooth_plane(field, smooth_x, smooth_y):
    along = jnp.einsum("ij,cpyj->cpyi", smooth_x, field, precision=lax.Precision.HIGHEST)
    return jnp.einsum("ij,cpjx->cpix", smooth_y, along, precision=lax.Precision.HIGHEST)


def diff_rows(field):
    zeros = jnp.zeros_like(field[..., :1, :])
    padded = jnp.concatenate([zeros, field, zeros], axis=-2)
    return (padded[..., 2:, :] - padded[..., :-2, :]) * 0.5


def rows_of(field, start, count):
    return lax.dynamic_slice_in_dim(field, start, count, field.ndim - 2)


def halve(field):
    high = field.astype(jnp.bfloat16)
    return high, (field - high.astype(jnp.float32)).astype(jnp.bfloat16)


def dot3(left, right):
    mul = lambda a, b: jnp.dot(a, b, preferred_element_type=jnp.float32)
    return mul(left[0], right[0]) + (mul(left[0], right[1]) + mul(left[1], right[0]))


def central(field, axis):
    size = field.shape[axis]
    place = lax.broadcasted_iota(jnp.int32, field.shape, axis)
    after = jnp.where(place == size - 1, 0.0, pltpu.roll(field, size - 1, axis))
    before = jnp.where(place == 0, 0.0, pltpu.roll(field, 1, axis))
    return (after - before) * 0.5


def plane_grads(plane, planes, below, here, above):
    over = jnp.where(plane == planes - 1, 0.0, above)
    under = jnp.where(plane == 0, 0.0, below)
    return central(here, 1), central(here, 0), (over - under) * 0.5


def smooth_fields(grads, moment, fields, matrices, store):
    rows_high, rows_low, cols_high, cols_low = matrices
    for at, grad in enumerate(grads):
        fields[at] = moment * grad

    @pl.loop(0, 3)
    def _(at):
        along = dot3((rows_high[...], rows_low[...]), halve(fields[at]))
        store(at, dot3(halve(along), (cols_high[...], cols_low[...])))


def split_matrices(rows_ref, cols_ref, matrices):
    matrices[0][...], matrices[1][...] = halve(rows_ref[...])
    matrices[2][...], matrices[3][...] = halve(cols_ref[...])


def chunk_kernel(low, count, planes, starts, *refs):
    chunks, refs = refs[: len(starts)], refs[len(starts) :]
    rows_ref, cols_ref, vel_out, images, moments, fields, sems = refs[:7]
    matrices = refs[7:]
    turn = pl.program_id(0)
    near = range(max(low - 1, 0), min(low + count + 1, planes))

    def place(plane):
        which = max(k for k, start in enumerate(starts) if start <= plane)
        return chunks[which], plane - starts[which]

    def image_copy(plane):
        chunk, at = place(plane)
        slot = plane - low + 1
        return pltpu.make_async_copy(chunk.at[0, at], images.at[slot], sems.at[0, slot])

    def moment_copy(plane):
        chunk, at = place(plane)
        slot = plane - low
        return pltpu.make_async_copy(chunk.at[1, at], moments.at[slot], sems.at[1, slot])

    @pl.when(turn == 0)
    def _():
        for plane in near:
            image_copy(plane).start()
            if low <= plane < low + count:
                moment_copy(plane).start()
        split_matrices(rows_ref, cols_ref, matrices)

    for step in range(count):

        @pl.when(turn == step)
        def _(step=step):
            for plane in near:
                if plane == low + step + 1 or (step == 0 and plane <= low):
                    image_copy(plane).wait()
            moment_copy(low + step).wait()

    grads = plane_grads(low + turn, planes, images[turn], images[turn + 1], images[turn + 2])

    def store(field, value):
        vel_out[field] = value

    smooth_fields(grads, moments[turn], fields, matrices, store)


def chunk_smooth(chunks, starts, low, count, planes, smooth_y, cols_matrix):
    rows, cols = chunks[0].shape[2:]
    return pl.pallas_call(
        functools.partial(chunk_kernel, low, count, planes, starts),
        grid=(count,),
        out_shape=jax.ShapeDtypeStruct((3, count, rows, cols), jnp.float32),
        in_specs=[pl.BlockSpec(memory_space=pl.ANY)] * len(chunks)
        + [whole_spec(smooth_y.shape), whole_spec(cols_matrix.shape)],
        out_specs=pl.BlockSpec((3, None, rows, cols), lambda at: (0, at, 0, 0)),
        scratch_shapes=[
            pltpu.VMEM((count + 2, rows, cols), jnp.float32),
            pltpu.VMEM((count, rows, cols), jnp.float32),
            pltpu.VMEM((3, rows, cols), jnp.float32),
            pltpu.SemaphoreType.DMA((2, count + 2)),
        ]
        + matrix_scratch(rows, rows, cols),
        cost_estimate=pl.CostEstimate(
            flops=36 * count * rows * rows * cols,
            bytes_accessed=20 * count * rows * cols,
            transcendentals=0,
        ),
        compiler_params=pltpu.CompilerParams(vmem_limit_bytes=40 * 2**20),
    )(*chunks, smooth_y, cols_matrix)


def shoot_kernel(planes, starts, parts, blocks, step, first_ref, smooth_z, *refs):
    chunks, refs = refs[: len(starts)], refs[len(starts) :]
    smoothed, refs = refs[: len(parts)], refs[len(parts) :]
    rows_ref, cols_ref, vel_out, image_out, moment_out = refs[:5]
    vel, images, moments, new_images, new_moments, fields, sems = refs[5:12]
    matrices = refs[12:]
    turn = pl.program_id(0)
    plane = turn - blocks
    rows = vel.shape[2]
    block = rows // blocks
    span = image_out.shape[0]

    def copies(at):
        which = max(k for k, start in enumerate(starts) if start <= at)
        inner, slot = at - starts[which], at % 4
        return [
            pltpu.make_async_copy(
                chunks[which].at[kind, inner], into.at[slot], sems.at[kind, slot]
            )
            for kind, into in enumerate((images, moments))
        ]

    @pl.when(turn == 0)
    def _():
        for at in range(min(2, planes)):
            for copy in copies(at):
                copy.start()
        split_matrices(rows_ref, cols_ref, matrices)

    @pl.when(turn < blocks)
    def _():
        @pl.loop(0, 3 * (block // 8))
        def _(part):
            field = part // (block // 8)
            inner = (part % (block // 8)) * 8
            held = [
                piece[field, j, pl.ds(pl.multiple_of(inner, 8), 8), :]
                for piece in smoothed
                for j in range(piece.shape[1])
            ]
            into = pl.ds(pl.multiple_of(turn * block + inner, 8), 8)
            for i in range(planes):
                vel[field, i, into, :] = -sum(smooth_z[i, j] * held[j] for j in range(planes))

    for at in range(planes):

        @pl.when(plane == at)
        def _(at=at):
            if at + 2 < planes:
                for copy in copies(at + 2):
                    copy.start()
            for near in ([0, 1] if at == 0 else [at + 1]):
                if near < planes:
                    for copy in copies(near):
                        copy.wait()

    @pl.when((plane >= 0) & (plane < planes))
    def _():
        here, above, below = plane % 4, (plane + 1) % 4, (plane + 3) % 4
        image, moment = images[here], moments[here]
        grads = plane_grads(plane, planes, images[below], image, images[above])
        moved = [vel[field, plane] for field in range(3)]
        new_images[plane % 3] = image - step * sum(v * g for v, g in zip(moved, grads))
        over = moments[above] * vel[2, jnp.minimum(plane + 1, planes - 1)]
        under = moments[below] * vel[2, jnp.maximum(plane - 1, 0)]
        over = jnp.where(plane == planes - 1, 0.0, over)
        under = jnp.where(plane == 0, 0.0, under)
        new_moments[plane % 2] = moment - step * (
            central(moment * moved[0], 1) + central(moment * moved[1], 0) + (over - under) * 0.5
        )

    @pl.when(plane >= 1)
    def _():
        last = plane - 1
        grads = plane_grads(
            last, planes, new_images[(last + 2) % 3], new_images[last % 3],
            new_images[(last + 1) % 3],
        )

        def store(field, value):
            vel_out[field] = value

        smooth_fields(grads, new_moments[last % 2], fields, matrices, store)
        window = pl.ds(pl.multiple_of(first_ref[0], 8), span)
        image_out[...] = new_images[last % 3, window, :]
        moment_out[...] = new_moments[last % 2, window, :]


def shoot(chunks, starts, smoothed, planes, smooth_z, rows_matrix, cols_matrix, first, step):
    rows, cols = chunks[0].shape[2:]
    span = rows_matrix.shape[0]
    blocks = max(1, rows // 64)
    block = rows // blocks
    parts = [piece.shape[1] for piece in smoothed]
    late = lambda at: jnp.clip(at - blocks - 1, 0, planes - 1)
    out = jax.ShapeDtypeStruct((planes, span, cols), jnp.float32)
    window = pl.BlockSpec((None, span, cols), lambda at: (late(at), 0, 0))
    return pl.pallas_call(
        functools.partial(shoot_kernel, planes, starts, parts, blocks, step),
        grid=(blocks + planes + 1,),
        out_shape=(jax.ShapeDtypeStruct((3, planes, span, cols), jnp.float32), out, out),
        in_specs=[pl.BlockSpec(memory_space=pltpu.SMEM)] * 2
        + [pl.BlockSpec(memory_space=pl.ANY)] * len(chunks)
        + [
            pl.BlockSpec(
                (3, part, block, cols), lambda at: (0, 0, jnp.minimum(at, blocks - 1), 0)
            )
            for part in parts
        ]
        + [whole_spec(rows_matrix.shape), whole_spec(cols_matrix.shape)],
        out_specs=(
            pl.BlockSpec((3, None, span, cols), lambda at: (0, late(at), 0, 0)),
            window,
            window,
        ),
        scratch_shapes=[
            pltpu.VMEM((3, planes, rows, cols), jnp.float32),
            pltpu.VMEM((4, rows, cols), jnp.float32),
            pltpu.VMEM((4, rows, cols), jnp.float32),
            pltpu.VMEM((3, rows, cols), jnp.float32),
            pltpu.VMEM((2, rows, cols), jnp.float32),
            pltpu.VMEM((3, rows, cols), jnp.float32),
            pltpu.SemaphoreType.DMA((2, 4)),
        ]
        + matrix_scratch(span, rows, cols),
        compiler_params=pltpu.CompilerParams(vmem_limit_bytes=VMEM_BYTES),
    )(first, smooth_z, *chunks, *smoothed, rows_matrix, cols_matrix)


def last_kernel(
    planes, own, step, inner_ref, smooth_z, smoothed, image_ref, moment_ref, templates, subjects,
    image_out, moment_out, update_out, vel,
):
    span = image_ref.shape[1]

    @pl.loop(0, 3 * (span // 8))
    def _(part):
        field = part // (span // 8)
        rows = pl.ds(pl.multiple_of((part % (span // 8)) * 8, 8), 8)
        held = [smoothed[field, j, rows, :] for j in range(planes)]
        for i in range(planes):
            vel[field, i, rows, :] = -sum(smooth_z[i, j] * held[j] for j in range(planes))

    inner = pl.ds(pl.multiple_of(inner_ref[0], 8), own)

    @pl.loop(0, planes)
    def _(plane):
        over_at, under_at = jnp.minimum(plane + 1, planes - 1), jnp.maximum(plane - 1, 0)
        image, moment = image_ref[plane], moment_ref[plane]
        grads = plane_grads(plane, planes, image_ref[under_at], image, image_ref[over_at])
        moved = [vel[field, plane] for field in range(3)]
        over = jnp.where(plane == planes - 1, 0.0, moment_ref[over_at] * vel[2, over_at])
        under = jnp.where(plane == 0, 0.0, moment_ref[under_at] * vel[2, under_at])
        vel[0, plane] = image - step * sum(v * g for v, g in zip(moved, grads))
        vel[1, plane] = moment - step * (
            central(moment * moved[0], 1) + central(moment * moved[1], 0) + (over - under) * 0.5
        )
        new_image = vel[0, plane, inner, :]
        image_out[0, plane] = new_image
        moment_out[0, plane] = vel[1, plane, inner, :]
        update_out[plane] = templates[0, plane] - learn_rate * (new_image - subjects[0, plane])


def last_step(smoothed, image, moment, templates, subjects, smooth_z, inner, step):
    planes, own = templates.shape[1:3]
    vmem = pl.BlockSpec(memory_space=pltpu.VMEM)
    out = jax.ShapeDtypeStruct(templates.shape, jnp.float32)
    return pl.pallas_call(
        functools.partial(last_kernel, planes, own, step),
        out_shape=(out, out, jax.ShapeDtypeStruct(templates.shape[1:], jnp.float32)),
        in_specs=[pl.BlockSpec(memory_space=pltpu.SMEM)] * 2 + [vmem] * 5,
        out_specs=(vmem, vmem, vmem),
        scratch_shapes=[pltpu.VMEM(smoothed.shape, jnp.float32)],
        compiler_params=pltpu.CompilerParams(vmem_limit_bytes=40 * 2**20),
    )(inner, smooth_z, smoothed, image, moment, templates, subjects)


def matrix_scratch(rows, inner, cols):
    kinds = [(rows, inner), (rows, inner), (cols, cols), (cols, cols)]
    return [pltpu.VMEM(kind, jnp.bfloat16) for kind in kinds]


def whole_spec(shape):
    return pl.BlockSpec(shape, lambda at: (0,) * len(shape), pipeline_mode=pl.Buffered(1))


def on_device_gathered(templates, momentum, subjects, smooth_x, smooth_y, smooth_z, owned_block):
    time_step = 1.0 / STEPS
    planes, own = templates.shape[1:3]
    total = smooth_y.shape[0]
    index = lax.axis_index("slab")
    ends = [planes * cut // 8 for cut in CUTS] + [planes]
    starts = [0] + ends[:-1]
    cols_matrix = smooth_x.T
    chunks, smoothed, done = [], [], 0
    for start, end in zip(starts, ends):
        both = jnp.concatenate([templates[:, start:end], momentum[:, start:end]], axis=0)
        chunks.append(lax.all_gather(both, "slab", axis=2, tiled=True))
    for at, end in enumerate(ends):
        ready = end if end == planes else end - 1
        smoothed.append(
            chunk_smooth(
                chunks[: at + 1], starts[: at + 1], done, ready - done, planes, smooth_y, cols_matrix
            )
        )
        done = ready
    span = own + 2 * EDGE
    first = jnp.clip(index * own - EDGE, 0, total - span).astype(jnp.int32)
    inner = (index * own - first).astype(jnp.int32)
    vel, image, moment = shoot(
        chunks, starts, smoothed, planes, smooth_z, rows_of(smooth_y, first, span), cols_matrix,
        first[None], time_step,
    )
    image, moment, update = last_step(
        vel, image, moment, templates, subjects, smooth_z, inner[None], time_step
    )
    return (image, moment) + pull(update, owned_block)


def on_device(templates, momentum, subjects, smooth_x, smooth_y, smooth_z, owned_block):
    time_step = 1.0 / STEPS
    image = templates[0]
    moment = momentum[0]
    for section in range(STEPS):
        image_rows = with_halo(image, (("slab", 1),), 1)
        grad_rows = (image_rows[:, 2:, :] - image_rows[:, :-2, :]) * 0.5
        grad_cols = diff_cols(image)
        grad_planes = diff_planes(image)
        pushing = smooth_planes(
            jnp.stack([moment * grad_cols, moment * grad_rows, moment * grad_planes]), smooth_z
        )
        plane_fields = lax.all_to_all(pushing, "slab", split_axis=1, concat_axis=2, tiled=True)
        plane_vel = -smooth_plane(plane_fields, smooth_x, smooth_y)
        velocity = lax.all_to_all(plane_vel, "slab", split_axis=2, concat_axis=1, tiled=True)
        flux_edge = with_halo(moment * velocity[1], (("slab", 1),), 1)
        flux_rows = (flux_edge[:, 2:, :] - flux_edge[:, :-2, :]) * 0.5
        new_image = image - time_step * (
            velocity[0] * grad_cols + velocity[1] * grad_rows + velocity[2] * grad_planes
        )
        new_moment = moment - time_step * (
            diff_cols(moment * velocity[0]) + flux_rows + diff_planes(moment * velocity[2])
        )
        image = new_image
        moment = new_moment
    return finish(image, moment, templates, subjects, owned_block)


def finish(image, moment, templates, subjects, owned_block):
    update = templates[0] - learn_rate * (image - subjects[0])
    return (image[None], moment[None]) + pull(update, owned_block)


def pull(update, owned_block):
    groups = lax.axis_size("grp")
    planes_all = update.shape[0]
    block_planes = planes_all // groups
    center = lax.psum(update, "grp") / groups
    owned_index = owned_block[lax.axis_index("grp")]
    owned_out = lax.dynamic_slice_in_dim(center, owned_index * block_planes, block_planes, 0)[None]
    new_template = update + pull_weight * (center - update)
    return (owned_out, new_template[None])


def solution(mesh):
    def body(*args):
        templates, smooth_y = args[0], args[4]
        gathered = 2 * 4 * templates.shape[1] * templates.shape[3] * smooth_y.shape[0]
        return (on_device_gathered if gathered <= GATHER_BYTES else on_device)(*args)

    return jax.shard_map(
        body,
        mesh=mesh,
        in_specs=(
            P("grp", None, "slab", None),
            P("grp", None, "slab", None),
            P("grp", None, "slab", None),
            P(),
            P(),
            P(),
            P(),
        ),
        out_specs=(
            P("grp", None, "slab", None),
            P("grp", None, "slab", None),
            P("grp", None, "slab", None),
            P("grp", None, "slab", None),
        ),
        check_vma=False,
    )
```

```python
import functools

import jax
import jax.numpy as jnp
from jax import lax
from jax.experimental import pallas as pl
from jax.experimental.pallas import tpu as pltpu
from jax.sharding import PartitionSpec as P

STEPS = 2
EDGE = 8
CUTS = (6,)
VMEM_BYTES = 60 * 2**20
GATHER_BYTES = 16 * 2**20


learn_rate = 0.5
pull_weight = 0.5


def with_halo(cells, sides, width):
    for axis, dim in sides:
        count = lax.axis_size(axis)
        ends = count - 1
        head = lax.slice_in_dim(cells, 0, width, axis=dim)
        tail = lax.slice_in_dim(cells, cells.shape[dim] - width, cells.shape[dim], axis=dim)
        cells = jnp.concatenate(
            [
                lax.ppermute(tail, axis, [(i, (i + 1) % count) for i in range(ends)]),
                cells,
                lax.ppermute(head, axis, [((i + 1) % count, i) for i in range(ends)]),
            ],
            axis=dim,
        )
    return cells


def diff_cols(field):
    zeros = jnp.zeros_like(field[..., :1])
    padded = jnp.concatenate([zeros, field, zeros], axis=-1)
    return (padded[..., 2:] - padded[..., :-2]) * 0.5


def diff_planes(field):
    zeros = jnp.zeros_like(field[..., :1, :, :])
    padded = jnp.concatenate([zeros, field, zeros], axis=-3)
    return (padded[..., 2:, :, :] - padded[..., :-2, :, :]) * 0.5


def smooth_planes(field, smooth_z):
    return jnp.einsum("ij,cjyx->ciyx", smooth_z, field, precision=lax.Precision.HIGHEST)


def smooth_plane(field, smooth_x, smooth_y):
    along = jnp.einsum("ij,cpyj->cpyi", smooth_x, field, precision=lax.Precision.HIGHEST)
    return jnp.einsum("ij,cpjx->cpix", smooth_y, along, precision=lax.Precision.HIGHEST)


def diff_rows(field):
    zeros = jnp.zeros_like(field[..., :1, :])
    padded = jnp.concatenate([zeros, field, zeros], axis=-2)
    return (padded[..., 2:, :] - padded[..., :-2, :]) * 0.5


def rows_of(field, start, count):
    return lax.dynamic_slice_in_dim(field, start, count, field.ndim - 2)


def halve(field):
    high = field.astype(jnp.bfloat16)
    return high, (field - high.astype(jnp.float32)).astype(jnp.bfloat16)


def dot3(left, right):
    mul = lambda a, b: jnp.dot(a, b, preferred_element_type=jnp.float32)
    rows = left[0].shape[0]
    if rows <= 128:
        both = mul(jnp.concatenate(left, axis=0), right[0])
        return both[:rows] + (mul(left[0], right[1]) + both[rows:])
    return mul(left[0], right[0]) + (mul(left[0], right[1]) + mul(left[1], right[0]))


def central(field, axis):
    size = field.shape[axis]
    place = lax.broadcasted_iota(jnp.int32, field.shape, axis)
    after = jnp.where(place == size - 1, 0.0, pltpu.roll(field, size - 1, axis))
    before = jnp.where(place == 0, 0.0, pltpu.roll(field, 1, axis))
    return (after - before) * 0.5


def plane_grads(plane, planes, below, here, above):
    over = jnp.where(plane == planes - 1, 0.0, above)
    under = jnp.where(plane == 0, 0.0, below)
    return central(here, 1), central(here, 0), (over - under) * 0.5


def smooth_fields(grads, moment, fields, matrices, store):
    rows_high, rows_low, cols_high, cols_low = matrices
    for at, grad in enumerate(grads):
        fields[at] = moment * grad

    @pl.loop(0, 3)
    def _(at):
        along = dot3((rows_high[...], rows_low[...]), halve(fields[at]))
        store(at, dot3(halve(along), (cols_high[...], cols_low[...])))


def split_matrices(rows_ref, cols_ref, matrices):
    matrices[0][...], matrices[1][...] = halve(rows_ref[...])
    matrices[2][...], matrices[3][...] = halve(cols_ref[...])


def chunk_kernel(low, count, planes, starts, *refs):
    chunks, refs = refs[: len(starts)], refs[len(starts) :]
    rows_ref, cols_ref, vel_out, images, moments, fields, sems = refs[:7]
    matrices = refs[7:]
    turn = pl.program_id(0)
    near = range(max(low - 1, 0), min(low + count + 1, planes))

    def place(plane):
        which = max(k for k, start in enumerate(starts) if start <= plane)
        return chunks[which], plane - starts[which]

    def image_copy(plane):
        chunk, at = place(plane)
        slot = plane - low + 1
        return pltpu.make_async_copy(chunk.at[0, at], images.at[slot], sems.at[0, slot])

    def moment_copy(plane):
        chunk, at = place(plane)
        slot = plane - low
        return pltpu.make_async_copy(chunk.at[1, at], moments.at[slot], sems.at[1, slot])

    @pl.when(turn == 0)
    def _():
        for plane in near:
            image_copy(plane).start()
            if low <= plane < low + count:
                moment_copy(plane).start()
        split_matrices(rows_ref, cols_ref, matrices)

    for step in range(count):

        @pl.when(turn == step)
        def _(step=step):
            for plane in near:
                if plane == low + step + 1 or (step == 0 and plane <= low):
                    image_copy(plane).wait()
            moment_copy(low + step).wait()

    grads = plane_grads(low + turn, planes, images[turn], images[turn + 1], images[turn + 2])

    def store(field, value):
        vel_out[field] = value

    smooth_fields(grads, moments[turn], fields, matrices, store)


def chunk_smooth(chunks, starts, low, count, planes, smooth_y, cols_matrix):
    rows, cols = chunks[0].shape[2:]
    return pl.pallas_call(
        functools.partial(chunk_kernel, low, count, planes, starts),
        grid=(count,),
        out_shape=jax.ShapeDtypeStruct((3, count, rows, cols), jnp.float32),
        in_specs=[pl.BlockSpec(memory_space=pl.ANY)] * len(chunks)
        + [whole_spec(smooth_y.shape), whole_spec(cols_matrix.shape)],
        out_specs=pl.BlockSpec((3, None, rows, cols), lambda at: (0, at, 0, 0)),
        scratch_shapes=[
            pltpu.VMEM((count + 2, rows, cols), jnp.float32),
            pltpu.VMEM((count, rows, cols), jnp.float32),
            pltpu.VMEM((3, rows, cols), jnp.float32),
            pltpu.SemaphoreType.DMA((2, count + 2)),
        ]
        + matrix_scratch(rows, rows, cols),
        cost_estimate=pl.CostEstimate(
            flops=36 * count * rows * rows * cols,
            bytes_accessed=20 * count * rows * cols,
            transcendentals=0,
        ),
        compiler_params=pltpu.CompilerParams(vmem_limit_bytes=VMEM_BYTES),
    )(*chunks, smooth_y, cols_matrix)


def shoot_kernel(planes, starts, parts, blocks, step, first_ref, smooth_z, *refs):
    chunks, refs = refs[: len(starts)], refs[len(starts) :]
    smoothed, refs = refs[: len(parts)], refs[len(parts) :]
    rows_ref, cols_ref, vel_out, image_out, moment_out = refs[:5]
    vel, images, moments, new_images, new_moments, fields, sems = refs[5:12]
    matrices = refs[12:]
    turn = pl.program_id(0)
    plane = turn - blocks
    rows = vel.shape[2]
    block = rows // blocks
    span = image_out.shape[0]

    def copies(at):
        which = max(k for k, start in enumerate(starts) if start <= at)
        inner, slot = at - starts[which], at % 4
        return [
            pltpu.make_async_copy(
                chunks[which].at[kind, inner], into.at[slot], sems.at[kind, slot]
            )
            for kind, into in enumerate((images, moments))
        ]

    @pl.when(turn == 0)
    def _():
        for at in range(min(2, planes)):
            for copy in copies(at):
                copy.start()
        split_matrices(rows_ref, cols_ref, matrices)

    @pl.when(turn < blocks)
    def _():
        @pl.loop(0, 3 * (block // 8))
        def _(part):
            field = part // (block // 8)
            inner = (part % (block // 8)) * 8
            held = [
                piece[field, j, pl.ds(pl.multiple_of(inner, 8), 8), :]
                for piece in smoothed
                for j in range(piece.shape[1])
            ]
            into = pl.ds(pl.multiple_of(turn * block + inner, 8), 8)
            for i in range(planes):
                vel[field, i, into, :] = -sum(smooth_z[i, j] * held[j] for j in range(planes))

    for at in range(planes):

        @pl.when(plane == at)
        def _(at=at):
            if at + 2 < planes:
                for copy in copies(at + 2):
                    copy.start()
            for near in ([0, 1] if at == 0 else [at + 1]):
                if near < planes:
                    for copy in copies(near):
                        copy.wait()

    @pl.when((plane >= 0) & (plane < planes))
    def _():
        here, above, below = plane % 4, (plane + 1) % 4, (plane + 3) % 4
        image, moment = images[here], moments[here]
        grads = plane_grads(plane, planes, images[below], image, images[above])
        moved = [vel[field, plane] for field in range(3)]
        new_images[plane % 3] = image - step * sum(v * g for v, g in zip(moved, grads))
        over = moments[above] * vel[2, jnp.minimum(plane + 1, planes - 1)]
        under = moments[below] * vel[2, jnp.maximum(plane - 1, 0)]
        over = jnp.where(plane == planes - 1, 0.0, over)
        under = jnp.where(plane == 0, 0.0, under)
        new_moments[plane % 2] = moment - step * (
            central(moment * moved[0], 1) + central(moment * moved[1], 0) + (over - under) * 0.5
        )

    @pl.when(plane >= 1)
    def _():
        last = plane - 1
        grads = plane_grads(
            last, planes, new_images[(last + 2) % 3], new_images[last % 3],
            new_images[(last + 1) % 3],
        )

        def store(field, value):
            vel_out[field] = value

        smooth_fields(grads, new_moments[last % 2], fields, matrices, store)
        window = pl.ds(pl.multiple_of(first_ref[0], 8), span)
        image_out[...] = new_images[last % 3, window, :]
        moment_out[...] = new_moments[last % 2, window, :]


def shoot(chunks, starts, smoothed, planes, smooth_z, rows_matrix, cols_matrix, first, step):
    rows, cols = chunks[0].shape[2:]
    span = rows_matrix.shape[0]
    blocks = max(1, rows // 64)
    block = rows // blocks
    parts = [piece.shape[1] for piece in smoothed]
    late = lambda at: jnp.clip(at - blocks - 1, 0, planes - 1)
    out = jax.ShapeDtypeStruct((planes, span, cols), jnp.float32)
    window = pl.BlockSpec((None, span, cols), lambda at: (late(at), 0, 0))
    return pl.pallas_call(
        functools.partial(shoot_kernel, planes, starts, parts, blocks, step),
        grid=(blocks + planes + 1,),
        out_shape=(jax.ShapeDtypeStruct((3, planes, span, cols), jnp.float32), out, out),
        in_specs=[pl.BlockSpec(memory_space=pltpu.SMEM)] * 2
        + [pl.BlockSpec(memory_space=pl.ANY)] * len(chunks)
        + [
            pl.BlockSpec(
                (3, part, block, cols), lambda at: (0, 0, jnp.minimum(at, blocks - 1), 0)
            )
            for part in parts
        ]
        + [whole_spec(rows_matrix.shape), whole_spec(cols_matrix.shape)],
        out_specs=(
            pl.BlockSpec((3, None, span, cols), lambda at: (0, late(at), 0, 0)),
            window,
            window,
        ),
        scratch_shapes=[
            pltpu.VMEM((3, planes, rows, cols), jnp.float32),
            pltpu.VMEM((4, rows, cols), jnp.float32),
            pltpu.VMEM((4, rows, cols), jnp.float32),
            pltpu.VMEM((3, rows, cols), jnp.float32),
            pltpu.VMEM((2, rows, cols), jnp.float32),
            pltpu.VMEM((3, rows, cols), jnp.float32),
            pltpu.SemaphoreType.DMA((2, 4)),
        ]
        + matrix_scratch(span, rows, cols),
        compiler_params=pltpu.CompilerParams(vmem_limit_bytes=VMEM_BYTES),
    )(first, smooth_z, *chunks, *smoothed, rows_matrix, cols_matrix)


def last_kernel(
    planes, own, step, inner_ref, smooth_z, smoothed, image_ref, moment_ref, templates, subjects,
    image_out, moment_out, update_out, vel,
):
    span = image_ref.shape[1]

    @pl.loop(0, 3 * (span // 8))
    def _(part):
        field = part // (span // 8)
        rows = pl.ds(pl.multiple_of((part % (span // 8)) * 8, 8), 8)
        held = [smoothed[field, j, rows, :] for j in range(planes)]
        for i in range(planes):
            vel[field, i, rows, :] = -sum(smooth_z[i, j] * held[j] for j in range(planes))

    inner = pl.ds(pl.multiple_of(inner_ref[0], 8), own)

    @pl.loop(0, planes)
    def _(plane):
        over_at, under_at = jnp.minimum(plane + 1, planes - 1), jnp.maximum(plane - 1, 0)
        image, moment = image_ref[plane], moment_ref[plane]
        grads = plane_grads(plane, planes, image_ref[under_at], image, image_ref[over_at])
        moved = [vel[field, plane] for field in range(3)]
        over = jnp.where(plane == planes - 1, 0.0, moment_ref[over_at] * vel[2, over_at])
        under = jnp.where(plane == 0, 0.0, moment_ref[under_at] * vel[2, under_at])
        vel[0, plane] = image - step * sum(v * g for v, g in zip(moved, grads))
        vel[1, plane] = moment - step * (
            central(moment * moved[0], 1) + central(moment * moved[1], 0) + (over - under) * 0.5
        )
        new_image = vel[0, plane, inner, :]
        image_out[0, plane] = new_image
        moment_out[0, plane] = vel[1, plane, inner, :]
        update_out[plane] = templates[0, plane] - learn_rate * (new_image - subjects[0, plane])


def last_step(smoothed, image, moment, templates, subjects, smooth_z, inner, step):
    planes, own = templates.shape[1:3]
    vmem = pl.BlockSpec(memory_space=pltpu.VMEM)
    out = jax.ShapeDtypeStruct(templates.shape, jnp.float32)
    return pl.pallas_call(
        functools.partial(last_kernel, planes, own, step),
        out_shape=(out, out, jax.ShapeDtypeStruct(templates.shape[1:], jnp.float32)),
        in_specs=[pl.BlockSpec(memory_space=pltpu.SMEM)] * 2 + [vmem] * 5,
        out_specs=(vmem, vmem, vmem),
        scratch_shapes=[pltpu.VMEM(smoothed.shape, jnp.float32)],
        compiler_params=pltpu.CompilerParams(vmem_limit_bytes=40 * 2**20),
    )(inner, smooth_z, smoothed, image, moment, templates, subjects)


def matrix_scratch(rows, inner, cols):
    kinds = [(rows, inner), (rows, inner), (cols, cols), (cols, cols)]
    return [pltpu.VMEM(kind, jnp.bfloat16) for kind in kinds]


def whole_spec(shape):
    return pl.BlockSpec(shape, lambda at: (0,) * len(shape), pipeline_mode=pl.Buffered(1))


def on_device_gathered(templates, momentum, subjects, smooth_x, smooth_y, smooth_z, owned_block):
    time_step = 1.0 / STEPS
    planes, own = templates.shape[1:3]
    total = smooth_y.shape[0]
    index = lax.axis_index("slab")
    ends = [planes * cut // 8 for cut in CUTS] + [planes]
    starts = [0] + ends[:-1]
    cols_matrix = smooth_x.T
    chunks, smoothed, done = [], [], 0
    for start, end in zip(starts, ends):
        both = jnp.concatenate([templates[:, start:end], momentum[:, start:end]], axis=0)
        chunks.append(lax.all_gather(both, "slab", axis=2, tiled=True))
    for at, end in enumerate(ends):
        ready = end if end == planes else end - 1
        smoothed.append(
            chunk_smooth(
                chunks[: at + 1], starts[: at + 1], done, ready - done, planes, smooth_y, cols_matrix
            )
        )
        done = ready
    span = own + 2 * EDGE
    first = jnp.clip(index * own - EDGE, 0, total - span).astype(jnp.int32)
    inner = (index * own - first).astype(jnp.int32)
    vel, image, moment = shoot(
        chunks, starts, smoothed, planes, smooth_z, rows_of(smooth_y, first, span), cols_matrix,
        first[None], time_step,
    )
    image, moment, update = last_step(
        vel, image, moment, templates, subjects, smooth_z, inner[None], time_step
    )
    return (image, moment) + pull(update, owned_block)


def on_device(templates, momentum, subjects, smooth_x, smooth_y, smooth_z, owned_block):
    time_step = 1.0 / STEPS
    image = templates[0]
    moment = momentum[0]
    for section in range(STEPS):
        image_rows = with_halo(image, (("slab", 1),), 1)
        grad_rows = (image_rows[:, 2:, :] - image_rows[:, :-2, :]) * 0.5
        grad_cols = diff_cols(image)
        grad_planes = diff_planes(image)
        pushing = smooth_planes(
            jnp.stack([moment * grad_cols, moment * grad_rows, moment * grad_planes]), smooth_z
        )
        plane_fields = lax.all_to_all(pushing, "slab", split_axis=1, concat_axis=2, tiled=True)
        plane_vel = -smooth_plane(plane_fields, smooth_x, smooth_y)
        velocity = lax.all_to_all(plane_vel, "slab", split_axis=2, concat_axis=1, tiled=True)
        flux_edge = with_halo(moment * velocity[1], (("slab", 1),), 1)
        flux_rows = (flux_edge[:, 2:, :] - flux_edge[:, :-2, :]) * 0.5
        new_image = image - time_step * (
            velocity[0] * grad_cols + velocity[1] * grad_rows + velocity[2] * grad_planes
        )
        new_moment = moment - time_step * (
            diff_cols(moment * velocity[0]) + flux_rows + diff_planes(moment * velocity[2])
        )
        image = new_image
        moment = new_moment
    return finish(image, moment, templates, subjects, owned_block)


def finish(image, moment, templates, subjects, owned_block):
    update = templates[0] - learn_rate * (image - subjects[0])
    return (image[None], moment[None]) + pull(update, owned_block)


def sum_groups(field, orders):
    groups = lax.axis_size("grp")
    share = field.shape[0] // len(orders)
    pieces = [field[at * share : (at + 1) * share] for at in range(len(orders))]
    for turn in range(len(orders[0])):
        sent = [
            lax.ppermute(piece, "grp", [(i, i ^ order[turn]) for i in range(groups)])
            for piece, order in zip(pieces, orders)
        ]
        pieces = [piece + got for piece, got in zip(pieces, sent)]
    return jnp.concatenate(pieces, axis=0)


def pull(update, owned_block):
    groups = lax.axis_size("grp")
    planes_all = update.shape[0]
    block_planes = planes_all // groups
    if groups == 4 and planes_all % 2 == 0:
        center = sum_groups(update, ((1, 2), (2, 1))) / groups
    else:
        center = lax.psum(update, "grp") / groups
    owned_index = owned_block[lax.axis_index("grp")]
    owned_out = lax.dynamic_slice_in_dim(center, owned_index * block_planes, block_planes, 0)[None]
    new_template = update + pull_weight * (center - update)
    return (owned_out, new_template[None])


def solution(mesh):
    def body(*args):
        templates, smooth_y = args[0], args[4]
        gathered = 2 * 4 * templates.shape[1] * templates.shape[3] * smooth_y.shape[0]
        return (on_device_gathered if gathered <= GATHER_BYTES else on_device)(*args)

    return jax.shard_map(
        body,
        mesh=mesh,
        in_specs=(
            P("grp", None, "slab", None),
            P("grp", None, "slab", None),
            P("grp", None, "slab", None),
            P(),
            P(),
            P(),
            P(),
        ),
        out_specs=(
            P("grp", None, "slab", None),
            P("grp", None, "slab", None),
            P("grp", None, "slab", None),
            P("grp", None, "slab", None),
        ),
        check_vma=False,
    )
```

```python
import functools

import jax
import jax.numpy as jnp
from jax import lax
from jax.experimental import pallas as pl
from jax.experimental.pallas import tpu as pltpu
from jax.sharding import PartitionSpec as P

STEPS = 2
EDGE = 8
CUTS = (6,)
VMEM_BYTES = 60 * 2**20
GATHER_BYTES = 16 * 2**20


learn_rate = 0.5
pull_weight = 0.5


def with_halo(cells, sides, width):
    for axis, dim in sides:
        count = lax.axis_size(axis)
        ends = count - 1
        head = lax.slice_in_dim(cells, 0, width, axis=dim)
        tail = lax.slice_in_dim(cells, cells.shape[dim] - width, cells.shape[dim], axis=dim)
        cells = jnp.concatenate(
            [
                lax.ppermute(tail, axis, [(i, (i + 1) % count) for i in range(ends)]),
                cells,
                lax.ppermute(head, axis, [((i + 1) % count, i) for i in range(ends)]),
            ],
            axis=dim,
        )
    return cells


def diff_cols(field):
    zeros = jnp.zeros_like(field[..., :1])
    padded = jnp.concatenate([zeros, field, zeros], axis=-1)
    return (padded[..., 2:] - padded[..., :-2]) * 0.5


def diff_planes(field):
    zeros = jnp.zeros_like(field[..., :1, :, :])
    padded = jnp.concatenate([zeros, field, zeros], axis=-3)
    return (padded[..., 2:, :, :] - padded[..., :-2, :, :]) * 0.5


def smooth_planes(field, smooth_z):
    return jnp.einsum("ij,cjyx->ciyx", smooth_z, field, precision=lax.Precision.HIGHEST)


def smooth_plane(field, smooth_x, smooth_y):
    along = jnp.einsum("ij,cpyj->cpyi", smooth_x, field, precision=lax.Precision.HIGHEST)
    return jnp.einsum("ij,cpjx->cpix", smooth_y, along, precision=lax.Precision.HIGHEST)


def diff_rows(field):
    zeros = jnp.zeros_like(field[..., :1, :])
    padded = jnp.concatenate([zeros, field, zeros], axis=-2)
    return (padded[..., 2:, :] - padded[..., :-2, :]) * 0.5


def rows_of(field, start, count):
    return lax.dynamic_slice_in_dim(field, start, count, field.ndim - 2)


def halve(field):
    high = field.astype(jnp.bfloat16)
    return high, (field - high.astype(jnp.float32)).astype(jnp.bfloat16)


def dot3(left, right):
    mul = lambda a, b: jnp.dot(a, b, preferred_element_type=jnp.float32)
    rows = left[0].shape[0]
    if rows <= 128:
        both = mul(jnp.concatenate(left, axis=0), right[0])
        return both[:rows] + (mul(left[0], right[1]) + both[rows:])
    return mul(left[0], right[0]) + (mul(left[0], right[1]) + mul(left[1], right[0]))


def central(field, axis):
    size = field.shape[axis]
    place = lax.broadcasted_iota(jnp.int32, field.shape, axis)
    after = jnp.where(place == size - 1, 0.0, pltpu.roll(field, size - 1, axis))
    before = jnp.where(place == 0, 0.0, pltpu.roll(field, 1, axis))
    return (after - before) * 0.5


def plane_grads(plane, planes, below, here, above):
    over = jnp.where(plane == planes - 1, 0.0, above)
    under = jnp.where(plane == 0, 0.0, below)
    return central(here, 1), central(here, 0), (over - under) * 0.5


def smooth_fields(grads, moment, fields, matrices, store):
    rows_high, rows_low, cols_high, cols_low = matrices
    for at, grad in enumerate(grads):
        fields[at] = moment * grad

    for at in range(3):
        along = dot3((rows_high[...], rows_low[...]), halve(fields[at]))
        store(at, dot3(halve(along), (cols_high[...], cols_low[...])))


def split_matrices(rows_ref, cols_ref, matrices):
    matrices[0][...], matrices[1][...] = halve(rows_ref[...])
    matrices[2][...], matrices[3][...] = halve(cols_ref[...])


def chunk_kernel(low, count, planes, starts, *refs):
    chunks, refs = refs[: len(starts)], refs[len(starts) :]
    rows_ref, cols_ref, vel_out, images, moments, fields, sems = refs[:7]
    matrices = refs[7:]
    turn = pl.program_id(0)
    near = range(max(low - 1, 0), min(low + count + 1, planes))

    def place(plane):
        which = max(k for k, start in enumerate(starts) if start <= plane)
        return chunks[which], plane - starts[which]

    def image_copy(plane):
        chunk, at = place(plane)
        slot = plane - low + 1
        return pltpu.make_async_copy(chunk.at[0, at], images.at[slot], sems.at[0, slot])

    def moment_copy(plane):
        chunk, at = place(plane)
        slot = plane - low
        return pltpu.make_async_copy(chunk.at[1, at], moments.at[slot], sems.at[1, slot])

    @pl.when(turn == 0)
    def _():
        for plane in near:
            image_copy(plane).start()
            if low <= plane < low + count:
                moment_copy(plane).start()
        split_matrices(rows_ref, cols_ref, matrices)

    for step in range(count):

        @pl.when(turn == step)
        def _(step=step):
            for plane in near:
                if plane == low + step + 1 or (step == 0 and plane <= low):
                    image_copy(plane).wait()
            moment_copy(low + step).wait()

    grads = plane_grads(low + turn, planes, images[turn], images[turn + 1], images[turn + 2])

    def store(field, value):
        vel_out[field] = value

    smooth_fields(grads, moments[turn], fields, matrices, store)


def chunk_smooth(chunks, starts, low, count, planes, smooth_y, cols_matrix):
    rows, cols = chunks[0].shape[2:]
    return pl.pallas_call(
        functools.partial(chunk_kernel, low, count, planes, starts),
        grid=(count,),
        out_shape=jax.ShapeDtypeStruct((3, count, rows, cols), jnp.float32),
        in_specs=[pl.BlockSpec(memory_space=pl.ANY)] * len(chunks)
        + [whole_spec(smooth_y.shape), whole_spec(cols_matrix.shape)],
        out_specs=pl.BlockSpec((3, None, rows, cols), lambda at: (0, at, 0, 0)),
        scratch_shapes=[
            pltpu.VMEM((count + 2, rows, cols), jnp.float32),
            pltpu.VMEM((count, rows, cols), jnp.float32),
            pltpu.VMEM((3, rows, cols), jnp.float32),
            pltpu.SemaphoreType.DMA((2, count + 2)),
        ]
        + matrix_scratch(rows, rows, cols),
        cost_estimate=pl.CostEstimate(
            flops=36 * count * rows * rows * cols,
            bytes_accessed=20 * count * rows * cols,
            transcendentals=0,
        ),
        compiler_params=pltpu.CompilerParams(vmem_limit_bytes=VMEM_BYTES),
    )(*chunks, smooth_y, cols_matrix)


def shoot_kernel(planes, starts, parts, blocks, step, first_ref, smooth_z, *refs):
    chunks, refs = refs[: len(starts)], refs[len(starts) :]
    smoothed, refs = refs[: len(parts)], refs[len(parts) :]
    rows_ref, cols_ref, vel_out, image_out, moment_out = refs[:5]
    vel, images, moments, new_images, new_moments, fields, sems = refs[5:12]
    matrices = refs[12:]
    turn = pl.program_id(0)
    plane = turn - blocks
    rows = vel.shape[2]
    block = rows // blocks
    span = image_out.shape[0]

    def copies(at):
        which = max(k for k, start in enumerate(starts) if start <= at)
        inner, slot = at - starts[which], at % 4
        return [
            pltpu.make_async_copy(
                chunks[which].at[kind, inner], into.at[slot], sems.at[kind, slot]
            )
            for kind, into in enumerate((images, moments))
        ]

    @pl.when(turn == 0)
    def _():
        for at in range(min(2, planes)):
            for copy in copies(at):
                copy.start()
        split_matrices(rows_ref, cols_ref, matrices)

    @pl.when(turn < blocks)
    def _():
        @pl.loop(0, 3 * (block // 8))
        def _(part):
            field = part // (block // 8)
            inner = (part % (block // 8)) * 8
            held = [
                piece[field, j, pl.ds(pl.multiple_of(inner, 8), 8), :]
                for piece in smoothed
                for j in range(piece.shape[1])
            ]
            into = pl.ds(pl.multiple_of(turn * block + inner, 8), 8)
            for i in range(planes):
                vel[field, i, into, :] = -sum(smooth_z[i, j] * held[j] for j in range(planes))

    for at in range(planes):

        @pl.when(plane == at)
        def _(at=at):
            if at + 2 < planes:
                for copy in copies(at + 2):
                    copy.start()
            for near in ([0, 1] if at == 0 else [at + 1]):
                if near < planes:
                    for copy in copies(near):
                        copy.wait()

    @pl.when((plane >= 0) & (plane < planes))
    def _():
        here, above, below = plane % 4, (plane + 1) % 4, (plane + 3) % 4
        image, moment = images[here], moments[here]
        grads = plane_grads(plane, planes, images[below], image, images[above])
        moved = [vel[field, plane] for field in range(3)]
        new_images[plane % 3] = image - step * sum(v * g for v, g in zip(moved, grads))
        over = moments[above] * vel[2, jnp.minimum(plane + 1, planes - 1)]
        under = moments[below] * vel[2, jnp.maximum(plane - 1, 0)]
        over = jnp.where(plane == planes - 1, 0.0, over)
        under = jnp.where(plane == 0, 0.0, under)
        new_moments[plane % 2] = moment - step * (
            central(moment * moved[0], 1) + central(moment * moved[1], 0) + (over - under) * 0.5
        )

    @pl.when(plane >= 1)
    def _():
        last = plane - 1
        grads = plane_grads(
            last, planes, new_images[(last + 2) % 3], new_images[last % 3],
            new_images[(last + 1) % 3],
        )

        def store(field, value):
            vel_out[field] = value

        smooth_fields(grads, new_moments[last % 2], fields, matrices, store)
        window = pl.ds(pl.multiple_of(first_ref[0], 8), span)
        image_out[...] = new_images[last % 3, window, :]
        moment_out[...] = new_moments[last % 2, window, :]


def shoot(chunks, starts, smoothed, planes, smooth_z, rows_matrix, cols_matrix, first, step):
    rows, cols = chunks[0].shape[2:]
    span = rows_matrix.shape[0]
    blocks = max(1, rows // 64)
    block = rows // blocks
    parts = [piece.shape[1] for piece in smoothed]
    late = lambda at: jnp.clip(at - blocks - 1, 0, planes - 1)
    out = jax.ShapeDtypeStruct((planes, span, cols), jnp.float32)
    window = pl.BlockSpec((None, span, cols), lambda at: (late(at), 0, 0))
    return pl.pallas_call(
        functools.partial(shoot_kernel, planes, starts, parts, blocks, step),
        grid=(blocks + planes + 1,),
        out_shape=(jax.ShapeDtypeStruct((3, planes, span, cols), jnp.float32), out, out),
        in_specs=[pl.BlockSpec(memory_space=pltpu.SMEM)] * 2
        + [pl.BlockSpec(memory_space=pl.ANY)] * len(chunks)
        + [
            pl.BlockSpec(
                (3, part, block, cols), lambda at: (0, 0, jnp.minimum(at, blocks - 1), 0)
            )
            for part in parts
        ]
        + [whole_spec(rows_matrix.shape), whole_spec(cols_matrix.shape)],
        out_specs=(
            pl.BlockSpec((3, None, span, cols), lambda at: (0, late(at), 0, 0)),
            window,
            window,
        ),
        scratch_shapes=[
            pltpu.VMEM((3, planes, rows, cols), jnp.float32),
            pltpu.VMEM((4, rows, cols), jnp.float32),
            pltpu.VMEM((4, rows, cols), jnp.float32),
            pltpu.VMEM((3, rows, cols), jnp.float32),
            pltpu.VMEM((2, rows, cols), jnp.float32),
            pltpu.VMEM((3, rows, cols), jnp.float32),
            pltpu.SemaphoreType.DMA((2, 4)),
        ]
        + matrix_scratch(span, rows, cols),
        compiler_params=pltpu.CompilerParams(vmem_limit_bytes=VMEM_BYTES),
    )(first, smooth_z, *chunks, *smoothed, rows_matrix, cols_matrix)


def last_kernel(
    planes, own, step, inner_ref, smooth_z, smoothed, image_ref, moment_ref, templates, subjects,
    image_out, moment_out, update_out, vel,
):
    span = image_ref.shape[1]

    @pl.loop(0, 3 * (span // 8))
    def _(part):
        field = part // (span // 8)
        rows = pl.ds(pl.multiple_of((part % (span // 8)) * 8, 8), 8)
        held = [smoothed[field, j, rows, :] for j in range(planes)]
        for i in range(planes):
            vel[field, i, rows, :] = -sum(smooth_z[i, j] * held[j] for j in range(planes))

    inner = pl.ds(pl.multiple_of(inner_ref[0], 8), own)

    @pl.loop(0, planes)
    def _(plane):
        over_at, under_at = jnp.minimum(plane + 1, planes - 1), jnp.maximum(plane - 1, 0)
        image, moment = image_ref[plane], moment_ref[plane]
        grads = plane_grads(plane, planes, image_ref[under_at], image, image_ref[over_at])
        moved = [vel[field, plane] for field in range(3)]
        over = jnp.where(plane == planes - 1, 0.0, moment_ref[over_at] * vel[2, over_at])
        under = jnp.where(plane == 0, 0.0, moment_ref[under_at] * vel[2, under_at])
        vel[0, plane] = image - step * sum(v * g for v, g in zip(moved, grads))
        vel[1, plane] = moment - step * (
            central(moment * moved[0], 1) + central(moment * moved[1], 0) + (over - under) * 0.5
        )
        new_image = vel[0, plane, inner, :]
        image_out[0, plane] = new_image
        moment_out[0, plane] = vel[1, plane, inner, :]
        update_out[plane] = templates[0, plane] - learn_rate * (new_image - subjects[0, plane])


def last_step(smoothed, image, moment, templates, subjects, smooth_z, inner, step):
    planes, own = templates.shape[1:3]
    vmem = pl.BlockSpec(memory_space=pltpu.VMEM)
    out = jax.ShapeDtypeStruct(templates.shape, jnp.float32)
    return pl.pallas_call(
        functools.partial(last_kernel, planes, own, step),
        out_shape=(out, out, jax.ShapeDtypeStruct(templates.shape[1:], jnp.float32)),
        in_specs=[pl.BlockSpec(memory_space=pltpu.SMEM)] * 2 + [vmem] * 5,
        out_specs=(vmem, vmem, vmem),
        scratch_shapes=[pltpu.VMEM(smoothed.shape, jnp.float32)],
        compiler_params=pltpu.CompilerParams(vmem_limit_bytes=40 * 2**20),
    )(inner, smooth_z, smoothed, image, moment, templates, subjects)


def matrix_scratch(rows, inner, cols):
    kinds = [(rows, inner), (rows, inner), (cols, cols), (cols, cols)]
    return [pltpu.VMEM(kind, jnp.bfloat16) for kind in kinds]


def whole_spec(shape):
    return pl.BlockSpec(shape, lambda at: (0,) * len(shape), pipeline_mode=pl.Buffered(1))


def on_device_gathered(templates, momentum, subjects, smooth_x, smooth_y, smooth_z, owned_block):
    time_step = 1.0 / STEPS
    planes, own = templates.shape[1:3]
    total = smooth_y.shape[0]
    index = lax.axis_index("slab")
    ends = [planes * cut // 8 for cut in CUTS] + [planes]
    starts = [0] + ends[:-1]
    cols_matrix = smooth_x.T
    chunks, smoothed, done = [], [], 0
    for start, end in zip(starts, ends):
        both = jnp.concatenate([templates[:, start:end], momentum[:, start:end]], axis=0)
        chunks.append(lax.all_gather(both, "slab", axis=2, tiled=True))
    for at, end in enumerate(ends):
        ready = end if end == planes else end - 1
        smoothed.append(
            chunk_smooth(
                chunks[: at + 1], starts[: at + 1], done, ready - done, planes, smooth_y, cols_matrix
            )
        )
        done = ready
    span = own + 2 * EDGE
    first = jnp.clip(index * own - EDGE, 0, total - span).astype(jnp.int32)
    inner = (index * own - first).astype(jnp.int32)
    vel, image, moment = shoot(
        chunks, starts, smoothed, planes, smooth_z, rows_of(smooth_y, first, span), cols_matrix,
        first[None], time_step,
    )
    image, moment, update = last_step(
        vel, image, moment, templates, subjects, smooth_z, inner[None], time_step
    )
    return (image, moment) + pull(update, owned_block)


def on_device(templates, momentum, subjects, smooth_x, smooth_y, smooth_z, owned_block):
    time_step = 1.0 / STEPS
    image = templates[0]
    moment = momentum[0]
    for section in range(STEPS):
        image_rows = with_halo(image, (("slab", 1),), 1)
        grad_rows = (image_rows[:, 2:, :] - image_rows[:, :-2, :]) * 0.5
        grad_cols = diff_cols(image)
        grad_planes = diff_planes(image)
        pushing = smooth_planes(
            jnp.stack([moment * grad_cols, moment * grad_rows, moment * grad_planes]), smooth_z
        )
        plane_fields = lax.all_to_all(pushing, "slab", split_axis=1, concat_axis=2, tiled=True)
        plane_vel = -smooth_plane(plane_fields, smooth_x, smooth_y)
        velocity = lax.all_to_all(plane_vel, "slab", split_axis=2, concat_axis=1, tiled=True)
        flux_edge = with_halo(moment * velocity[1], (("slab", 1),), 1)
        flux_rows = (flux_edge[:, 2:, :] - flux_edge[:, :-2, :]) * 0.5
        new_image = image - time_step * (
            velocity[0] * grad_cols + velocity[1] * grad_rows + velocity[2] * grad_planes
        )
        new_moment = moment - time_step * (
            diff_cols(moment * velocity[0]) + flux_rows + diff_planes(moment * velocity[2])
        )
        image = new_image
        moment = new_moment
    return finish(image, moment, templates, subjects, owned_block)


def finish(image, moment, templates, subjects, owned_block):
    update = templates[0] - learn_rate * (image - subjects[0])
    return (image[None], moment[None]) + pull(update, owned_block)


def sum_groups(field, orders):
    groups = lax.axis_size("grp")
    share = field.shape[0] // len(orders)
    pieces = [field[at * share : (at + 1) * share] for at in range(len(orders))]
    for turn in range(len(orders[0])):
        sent = [
            lax.ppermute(piece, "grp", [(i, i ^ order[turn]) for i in range(groups)])
            for piece, order in zip(pieces, orders)
        ]
        pieces = [piece + got for piece, got in zip(pieces, sent)]
    return jnp.concatenate(pieces, axis=0)


def pull(update, owned_block):
    groups = lax.axis_size("grp")
    planes_all = update.shape[0]
    block_planes = planes_all // groups
    if groups == 4 and planes_all % 2 == 0:
        center = sum_groups(update, ((1, 2), (2, 1))) / groups
    else:
        center = lax.psum(update, "grp") / groups
    owned_index = owned_block[lax.axis_index("grp")]
    owned_out = lax.dynamic_slice_in_dim(center, owned_index * block_planes, block_planes, 0)[None]
    new_template = update + pull_weight * (center - update)
    return (owned_out, new_template[None])


def solution(mesh):
    def body(*args):
        templates, smooth_y = args[0], args[4]
        gathered = 2 * 4 * templates.shape[1] * templates.shape[3] * smooth_y.shape[0]
        return (on_device_gathered if gathered <= GATHER_BYTES else on_device)(*args)

    return jax.shard_map(
        body,
        mesh=mesh,
        in_specs=(
            P("grp", None, "slab", None),
            P("grp", None, "slab", None),
            P("grp", None, "slab", None),
            P(),
            P(),
            P(),
            P(),
        ),
        out_specs=(
            P("grp", None, "slab", None),
            P("grp", None, "slab", None),
            P("grp", None, "slab", None),
            P("grp", None, "slab", None),
        ),
        check_vma=False,
    )
```
